256 devices in a mesh: band: 64 (over x, z, core), segment: 4 (over y).
Axes of the slice: x: 4, y: 4, z: 8, core: 2. Of those that a mesh axis runs over, the one named last changes fastest.
Arguments:
- fields: bfloat16 [8, 1024, 64, 256], P(None, 'band'), may hold values from -6 to 6
- land_sea: int32 [1024, 64], P('band'), may hold values from 0 to 1, as said below
- conv_kernel: bfloat16 [4, 7, 7, 256], P('segment'), may hold values from -0.875 to 0.875
- conv_bias: bfloat16 [4, 256], P('segment'), may hold values from -3 to 3
- norm_gain: bfloat16 [4, 256], P('segment'), may hold values from 0.5 to 1.5
- norm_shift: bfloat16 [4, 256], P('segment'), may hold values from -3 to 3
- up_proj: bfloat16 [4, 256, 1024], P('segment'), may hold values from -0.375 to 0.375
- up_bias: bfloat16 [4, 1024], P('segment'), may hold values from -3 to 3
- down_proj: bfloat16 [4, 1024, 256], P('segment'), may hold values from -0.1875 to 0.1875
- down_bias: bfloat16 [4, 256], P('segment'), may hold values from -3 to 3
Outputs:
- segment_out: bfloat16 [4, 8, 1024, 64, 256], P('segment', None, 'band')
The draws below stay inside these ranges and needn't reach their ends.
Inputs may be any that keep to these rules, and one draw needn't show every extreme that they name: `land_sea`: each index of band's 16 x 64 cells hold at most 768 wet cells, and some index holds exactly 768.
All inputs are finite; a program needn't handle non-finite values.
Results may differ from the reference program's by a relative error of at most 0.01.
Values may be sent and summed in bfloat16 or wider, within the bound.
A program may use at most 64 MiB of HBM per device.

```python
import jax
import jax.numpy as jnp
from jax import lax

C = 256
HID = 1024
KS = 7
R = 16
W = 64
MB = 8
H = 1024
CAP = 768
N_SEGMENT = 4


def permute_one(perm_key):
    return jax.random.permutation(perm_key, R * W)


def draw_land_sea(key, part):
    band_count = H // R
    count_key, pick_key, perm_key = jax.random.split(key, 3)
    wet_counts = jax.random.randint(count_key, (band_count,), R, CAP + 1)
    chosen = jax.random.randint(pick_key, (), 0, band_count)
    wet_counts = jnp.where(jnp.arange(band_count) == chosen, CAP, wet_counts)
    ranking = jax.vmap(permute_one)(jax.random.split(perm_key, band_count))
    wet_cells = (ranking < wet_counts[:, None]).astype(jnp.int32)
    return wet_cells.reshape(H, W)


def levels(rng, dims, cuts, least, high):
    loudness, own = 1.0, jax.random.fold_in(rng, 6)
    for position, shards_of in cuts:
        steps = jnp.exp(jax.random.uniform(jax.random.fold_in(own, position), (shards_of,), jnp.float32, least / len(cuts), high / len(cuts)))
        loudness = loudness * jnp.repeat(steps, dims[position] // shards_of).reshape([-1 if axis == position else 1 for axis in range(len(dims))])
    return loudness


def noise(rng, dims, scale, bound, cuts=(), dtype=jnp.bfloat16):
    factor_of = levels(rng, dims, cuts, -0.22, 0.18) if cuts else 1.0
    entries = jax.random.normal(rng, dims, jnp.float32) * scale * factor_of
    return jnp.minimum(jnp.maximum(entries, -bound), bound).astype(dtype)


def setup_inputs(seed: int = 0) -> dict:
    keys = jax.random.split(jax.random.key(seed), 11)
    fields = noise(keys[0], (MB, H, W, C), 1.0, 6.0, ((1, 64),))
    land_sea = draw_land_sea(jax.random.fold_in(keys[10], 71), 0)
    conv_kernel = noise(keys[2], (N_SEGMENT, KS, KS, C), (KS * KS) ** -0.5, 0.875, ((0, 4),))
    conv_bias = noise(keys[3], (N_SEGMENT, C), 0.5, 3.0, ((0, 4),))
    norm_gain = jnp.clip(0.5 + 1.0 * jax.random.uniform(keys[4], (N_SEGMENT, C), jnp.float32) ** levels(keys[4], (N_SEGMENT, C), ((0, 4),), -0.2, 0.2), 0.5, 1.5).astype(jnp.bfloat16)
    norm_shift = noise(keys[5], (N_SEGMENT, C), 0.5, 3.0, ((0, 4),))
    up_proj = noise(keys[6], (N_SEGMENT, C, HID), C ** -0.5, 0.375, ((0, 4),))
    up_bias = noise(keys[7], (N_SEGMENT, HID), 0.5, 3.0, ((0, 4),))
    down_proj = noise(keys[8], (N_SEGMENT, HID, C), HID ** -0.5, 0.1875, ((0, 4),))
    down_bias = noise(keys[9], (N_SEGMENT, C), 0.5, 3.0, ((0, 4),))
    return {"fields": fields, "land_sea": land_sea, "conv_kernel": conv_kernel, "conv_bias": conv_bias, "norm_gain": norm_gain, "norm_shift": norm_shift, "up_proj": up_proj, "up_bias": up_bias, "down_proj": down_proj, "down_bias": down_bias}


def layer_norm(summed, gain, offset):
    centre = lax.optimization_barrier(jnp.mean(summed, axis=-1, keepdims=True))
    deviation = summed - centre
    variance = lax.optimization_barrier(jnp.mean(deviation * deviation, axis=-1, keepdims=True))
    return deviation * lax.rsqrt(variance + 1e-06) * gain.astype(jnp.float32) + offset.astype(jnp.float32)

def section(state, mask, kernel, conv_b, norm_g, norm_o, up_w, up_b, down_w, down_b):
    row_count, col_count, channels = state.shape
    reach = kernel.shape[0] // 2
    padded_rows = jnp.pad(state, ((reach, reach), (0, 0), (0, 0)))
    wrapped = jnp.concatenate([padded_rows[:, col_count - reach:], padded_rows, padded_rows[:, :reach]], axis=1)
    summed = jnp.zeros(state.shape, jnp.float32) + conv_b.astype(jnp.float32)
    for row_off in range(2 * reach + 1):
        for col_off in range(2 * reach + 1):
            window = wrapped[row_off:row_off + row_count, col_off:col_off + col_count]
            summed = summed + window.astype(jnp.float32) * kernel[row_off, col_off].astype(jnp.float32)
    normed = layer_norm(summed, norm_g, norm_o).astype(jnp.bfloat16).reshape(row_count * col_count, channels)
    hidden = jax.nn.gelu(jnp.dot(normed, up_w, preferred_element_type=jnp.float32) + up_b.astype(jnp.float32), approximate=False).astype(jnp.bfloat16)
    update = jnp.dot(hidden, down_w, preferred_element_type=jnp.float32) + down_b.astype(jnp.float32)
    merged = (state.astype(jnp.float32) + update.reshape(state.shape)) * mask[:, :, None]
    return merged.astype(jnp.bfloat16)

def reference(fields, land_sea, conv_kernel, conv_bias, norm_gain, norm_shift, up_proj, up_bias, down_proj, down_bias):
    mask = land_sea.astype(jnp.float32)

    def run_one(field):
        state = (field.astype(jnp.float32) * mask[:, :, None]).astype(jnp.bfloat16)
        results = []
        for level in range(N_SEGMENT):
            state = section(state, mask, conv_kernel[level], conv_bias[level], norm_gain[level], norm_shift[level], up_proj[level], up_bias[level], down_proj[level], down_bias[level])
            results.append(state)
        return jnp.stack(results)
    stacked = lax.map(run_one, fields)
    return jnp.transpose(stacked, (1, 0, 2, 3, 4))
```

```python
import jax
import jax.numpy as jnp
from jax import lax
from jax.experimental import pallas as pl
from jax.experimental.pallas import tpu as pltpu
from jax.sharding import PartitionSpec as P

BF, F32 = jnp.bfloat16, jnp.float32
MESH = pl.DeviceIdType.MESH
KS, REACH = 7, 3
R, W, C, HID = 16, 64, 256, 1024
BLOCKS, DATES, BANDS = 4, 2, 64
PIECES = 8
UPR, DNR = C // PIECES, HID // PIECES
CH = 4
NCH = R // CH


def tree(p):
    return ((p[0] + p[1]) + (p[2] + p[3])) + ((p[4] + p[5]) + p[6])


def conv_row(state, taps, sp, normed, i):
    xs = [state[i + a].reshape(W // 8, 8, C) for a in range(KS)]
    acc = None
    for b in range(KS):
        t = tree([xs[a] * taps[a * KS + b][None] for a in range(KS)])
        t = t.astype(F32).reshape(W, C)
        if b != REACH:
            t = pltpu.roll(t, (REACH - b) % W, 0)
        acc = t if acc is None else acc + t
    summed = acc + sp[0:1, 0:C]
    mean = jnp.sum(summed, -1, keepdims=True) * (1.0 / C)
    dev = summed - mean
    var = jnp.sum(dev * dev, -1, keepdims=True) * (1.0 / C)
    out = dev * lax.rsqrt(var + 1e-6) * sp[1:2, 0:C] + sp[2:3, 0:C]
    normed[pl.ds(pl.multiple_of(i * W, W), W), :] = out.astype(BF)


def mlp_chunk(normed, state, result, mask, up, dn, sp, hid, ck):
    m = CH * W
    r0 = pl.multiple_of(ck * m, m)
    n = normed[pl.ds(r0, m), :]
    for j in range(4):
        js = slice(j * 256, (j + 1) * 256)
        h = jnp.dot(n, up[:, js], preferred_element_type=F32) + sp[4:5, js]
        v = h.astype(BF)
        e = lax.erf(v * jnp.asarray(0.7071067811865476, BF))
        hid[:, js] = v + v * e
    u = jnp.dot(hid[...], dn[...], preferred_element_type=F32) * 0.5 + sp[3:4, 0:C]
    st = state[pl.ds(ck * CH + REACH, CH)].reshape(m, C).astype(F32)
    mk = mask[pl.ds(r0, m), :]
    o = (st + u) * jnp.concatenate([mk, mk], axis=1)
    result[pl.ds(ck * CH + REACH, CH)] = o.astype(BF).reshape(CH, W, C)


def kernel(fields, land, ck, cb, ng, ns, up, ub, dn, db, out,
           S, WU, WD, CK, SP, TP, N, H, MK,
           f_sem, own_sem, y_send, k_send, k_recv, w_recv, x_send, c_send,
           h_send, h_recv, o_send, o_recv, l_sem):
    band, q = lax.axis_index("band"), lax.axis_index("segment")
    core = lax.rem(band, 2)
    xpos = band // 16
    sib = band + 1 - 2 * core
    other = jnp.where(core == 0, band - 1, band + 1)
    has_prev, has_next = band > 0, band < BANDS - 1
    has_other = jnp.logical_and(other >= 0, other < BANDS)
    mine = 2 * xpos + core

    def at(b, s):
        return {"band": b, "segment": s}

    def x_band(k):
        return lax.rem(band + 16 * k, BANDS)

    def seg(r):
        return lax.rem(q + r, BLOCKS)

    barrier = pltpu.get_barrier_semaphore()

    def greet(b, s):
        pl.semaphore_signal(barrier, inc=1, device_id=at(b, s), device_id_type=MESH)

    for r in (1, 2, 3):
        greet(band, seg(r))
    for k in (1, 2, 3):
        greet(x_band(k), q)
    greet(sib, q)

    @pl.when(has_other)
    def _():
        greet(other, q)

    def field_copy(d):
        return pltpu.make_async_copy(
            fields.at[DATES * q + d], S.at[d, 0, pl.ds(REACH, R)], f_sem.at[d])

    field_copy(0).start()
    field_copy(1).start()
    own_up = pltpu.make_async_copy(up.at[0], WU.at[q], own_sem.at[0])
    own_dn = pltpu.make_async_copy(dn.at[0], WD.at[q], own_sem.at[1])
    own_up.start()
    own_dn.start()

    CK[q] = ck[0]
    SP[q, 0:1, 0:C] = cb[...].astype(F32)
    SP[q, 1:2, 0:C] = ng[...].astype(F32)
    SP[q, 2:3, 0:C] = ns[...].astype(F32)
    SP[q, 3:4, 0:C] = db[...].astype(F32)
    SP[q, 4:5, :] = ub[...].astype(F32)

    eye = (lax.broadcasted_iota(jnp.int32, (W, W), 0)
           == lax.broadcasted_iota(jnp.int32, (W, W), 1))

    @pl.loop(0, R)
    def _(i):
        row = jnp.broadcast_to(land[pl.ds(i, 1), :].astype(F32), (W, W))
        col = jnp.sum(jnp.where(eye, row, 0.0), -1, keepdims=True)
        MK[pl.ds(pl.multiple_of(i * W, W), W), :] = jnp.broadcast_to(col, (W, 128))

    edge = jnp.zeros((REACH, W, C), BF)

    @pl.when(jnp.logical_not(has_prev))
    def _():
        @pl.loop(0, DATES * BLOCKS)
        def _(t):
            S[t // BLOCKS, lax.rem(t, BLOCKS), 0:REACH] = edge

    @pl.when(jnp.logical_not(has_next))
    def _():
        @pl.loop(0, DATES * BLOCKS)
        def _(t):
            S[t // BLOCKS, lax.rem(t, BLOCKS), R + REACH:R + 2 * REACH] = edge

    pl.semaphore_wait(barrier, 7 + has_other.astype(jnp.int32))

    def k_copies(r, s):
        return (
            pltpu.make_async_remote_copy(
                CK.at[s], CK.at[s], k_send.at[r - 1, 0], k_recv.at[s, 0],
                device_id=at(band, seg(r)), device_id_type=MESH),
            pltpu.make_async_remote_copy(
                SP.at[s], SP.at[s], k_send.at[r - 1, 1], k_recv.at[s, 1],
                device_id=at(band, seg(r)), device_id_type=MESH))

    def part(ref, s, p, w):
        n = (UPR, DNR)[w]
        return ref.at[s, pl.ds(pl.multiple_of(p * n, n), n)]

    def y_copy(r, w):
        return pltpu.make_async_remote_copy(
            part((up, dn)[w], 0, mine, w), part((WU, WD)[w], q, mine, w),
            y_send.at[r - 1, w], w_recv.at[q, mine, w],
            device_id=at(band, seg(r)), device_id_type=MESH)

    def w_copy(s, p, w, b, sem):
        ref = (WU, WD)[w]
        return pltpu.make_async_remote_copy(
            part(ref, s, p, w), part(ref, s, p, w), sem, w_recv.at[s, p, w],
            device_id=at(b, q), device_id_type=MESH)

    def x_copy(s, k, w):
        return w_copy(s, mine, w, x_band(k), x_send.at[s, k - 1, w])

    def c_copy(s, k, w):
        p = 2 * lax.rem(xpos + k, 4) + core
        return w_copy(s, p, w, sib, c_send.at[s, k, w])

    for r in (1, 3, 2):
        for c in k_copies(r, q):
            c.start()
    for w in (0, 1):
        for r in (1, 3, 2):
            y_copy(r, w).start()

    def stage_x(s):
        @pl.when(q != s)
        def _():
            for w in (0, 1):
                c_copy(s, 0, w).wait_recv()
                for k in (1, 3, 2):
                    x_copy(s, k, w).start()
                c_copy(s, 0, w).start()

    def stage_c(s):
        @pl.when(q != s)
        def _():
            for w in (0, 1):
                for k in (1, 3, 2):
                    c_copy(s, k, w).wait_recv()
                    c_copy(s, k, w).start()

    def stage_f(s):
        @pl.when(q != s)
        def _():
            for w in (0, 1):
                for k in range(4):
                    p = 2 * k + 1 - core
                    w_copy(s, p, w, sib, c_send.at[s, k, w]).wait_recv()

        @pl.when(q == s)
        def _():
            own_up.wait()
            own_dn.wait()

    def halo(d, s, side):
        src = pl.ds(REACH, REACH) if side == 0 else pl.ds(R, REACH)
        dst = pl.ds(R + REACH, REACH) if side == 0 else pl.ds(0, REACH)
        to = band - 1 if side == 0 else band + 1
        return pltpu.make_async_remote_copy(
            S.at[d, s, src], S.at[d, s, dst], h_send.at[d, s, side], h_recv.at[d, s, side],
            device_id=at(to, q), device_id_type=MESH)

    def halo_start(d, s):
        @pl.when(has_prev)
        def _():
            halo(d, s, 0).start()

        @pl.when(has_next)
        def _():
            halo(d, s, 1).start()

    def halo_wait(d, s):
        @pl.when(has_next)
        def _():
            halo(d, s, 0).wait_recv()

        @pl.when(has_prev)
        def _():
            halo(d, s, 1).wait_recv()

    def halo_done(d, s):
        @pl.when(has_prev)
        def _():
            halo(d, s, 0).wait_send()

        @pl.when(has_next)
        def _():
            halo(d, s, 1).wait_send()

    for d in range(DATES):
        field_copy(d).wait()

        @pl.loop(0, R)
        def _(i):
            m = MK[pl.ds(pl.multiple_of(i * W, W), W), :]
            x = S[d, 0, i + REACH].astype(F32) * jnp.concatenate([m, m], axis=1)
            S[d, 0, i + REACH] = x.astype(BF)

        halo_start(d, 0)

    def rows(ref, ck):
        return ref.at[pl.ds(ck * CH, CH)]

    def o_copy(d, s, ck):
        return pltpu.make_async_remote_copy(
            S.at[d, s + 1, pl.ds(REACH + ck * CH, CH)],
            out.at[0, DATES * q + d, pl.ds(ck * CH, CH)],
            o_send.at[d, s, ck], o_recv.at[DATES * q + d, ck],
            device_id=at(band, s), device_id_type=MESH)

    def l_copy(d, s, ck):
        return pltpu.make_async_copy(
            S.at[d, s + 1, pl.ds(REACH + ck * CH, CH)],
            out.at[0, DATES * q + d, pl.ds(ck * CH, CH)], l_sem.at[d, ck])

    def send_out(d, s, ck):
        @pl.when(q != s)
        def _():
            o_copy(d, s, ck).start()

        @pl.when(q == s)
        def _():
            l_copy(d, s, ck).start()

    def order(t):
        return jnp.where(t == 1, NCH - 1, jnp.where(t > 1, t - 1, 0))

    @pl.loop(0, DATES * BLOCKS)
    def _(unit):
        d, s = unit // BLOCKS, lax.rem(unit, BLOCKS)
        state, result = S.at[d, s], S.at[d, s + 1]
        taps, sp, wu, wd = TP.at[s], SP.at[s], WU.at[s], WD.at[s]

        @pl.when(d == 0)
        def _():
            @pl.when(q != s)
            def _():
                for w in (0, 1):
                    pltpu.make_async_remote_copy(
                        (CK, SP)[w].at[s], (CK, SP)[w].at[s], k_send.at[0, w], k_recv.at[s, w],
                        device_id=at(band, seg(1)), device_id_type=MESH).wait_recv()

            @pl.loop(0, KS)
            def _(a):
                line = CK[s, a].astype(F32)
                for b in range(KS):
                    taps[a * KS + b] = jnp.broadcast_to(line[b:b + 1], (8, C)).astype(BF)

        @pl.loop(0, 5)
        def _(t):
            conv_row(state, taps, sp, N, 2 * t + 3)
            conv_row(state, taps, sp, N, 2 * t + 4)

        halo_wait(d, s)

        @pl.loop(0, 3)
        def _(t):
            conv_row(state, taps, sp, N, t)
            conv_row(state, taps, sp, N, t + 13)

        @pl.when(d == 0)
        def _():
            @pl.when(s == 0)
            def _():
                stage_x(0)
                stage_c(0)
            stage_f(s)

            @pl.when(s < BLOCKS - 1)
            def _():
                stage_x(s + 1)

        @pl.loop(0, NCH)
        def _(t):
            mlp_chunk(N, state, result, MK, wu, wd, sp, H, order(t))

            @pl.when(jnp.logical_and(t == 1, s < BLOCKS - 1))
            def _():
                halo_start(d, s + 1)

            @pl.when(t > 0)
            def _():
                send_out(d, s, order(t - 1))

        @pl.when(jnp.logical_and(d == 0, s < BLOCKS - 1))
        def _():
            stage_c(s + 1)

        send_out(d, s, order(NCH - 1))

    for r in (1, 2, 3):
        for c in k_copies(r, q):
            c.wait_send()
        for w in (0, 1):
            y_copy(r, w).wait_send()

    @pl.loop(0, BLOCKS)
    def _(s):
        @pl.when(q != s)
        def _():
            for w in (0, 1):
                for k in (1, 2, 3):
                    x_copy(s, k, w).wait_send()
                for k in range(4):
                    c_copy(s, k, w).wait_send()

        for d in range(DATES):
            halo_done(d, s)

            @pl.when(q != s)
            def _():
                for t in range(NCH):
                    o_copy(d, s, t).wait_send()

            @pl.when(q == s)
            def _():
                for t in range(NCH):
                    l_copy(d, s, t).wait()

        @pl.when(q != s)
        def _():
            for d in range(DATES):
                for t in range(NCH):
                    pltpu.make_async_remote_copy(
                        S.at[d, 1, pl.ds(REACH + t * CH, CH)],
                        out.at[0, DATES * s + d, pl.ds(t * CH, CH)],
                        o_send.at[d, 0, t], o_recv.at[DATES * s + d, t],
                        device_id=at(band, s), device_id_type=MESH).wait_recv()


def on_device(*args):
    any_, vmem = pl.BlockSpec(memory_space=pl.ANY), pl.BlockSpec(memory_space=pltpu.VMEM)
    dma = pltpu.SemaphoreType.DMA
    return pl.pallas_call(
        kernel,
        out_shape=jax.ShapeDtypeStruct((1, DATES * BLOCKS, R, W, C), BF),
        in_specs=[any_, vmem, vmem, vmem, vmem, vmem, any_, vmem, any_, vmem],
        out_specs=any_,
        scratch_shapes=[
            pltpu.VMEM((DATES, BLOCKS + 1, R + 2 * REACH, W, C), BF),
            pltpu.VMEM((BLOCKS, C, HID), BF),
            pltpu.VMEM((BLOCKS, HID, C), BF),
            pltpu.VMEM((BLOCKS, KS, KS, C), BF),
            pltpu.VMEM((BLOCKS, 8, HID), F32),
            pltpu.VMEM((BLOCKS, KS * KS, 8, C), BF),
            pltpu.VMEM((R * W, C), BF),
            pltpu.VMEM((CH * W, HID), BF),
            pltpu.VMEM((R * W, 128), F32),
            dma((DATES,)),
            dma((2,)),
            dma((3, 2)),
            dma((3, 2)),
            dma((BLOCKS, 2)),
            dma((BLOCKS, PIECES, 2)),
            dma((BLOCKS, 3, 2)),
            dma((BLOCKS, 4, 2)),
            dma((DATES, BLOCKS, 2)),
            dma((DATES, BLOCKS, 2)),
            dma((DATES, BLOCKS, NCH)),
            dma((DATES * BLOCKS, NCH)),
            dma((DATES, NCH)),
        ],
        compiler_params=pltpu.CompilerParams(collective_id=0, has_side_effects=True),
        name="blocks",
    )(*args)


def solution(mesh):
    in_specs = (
        P(None, "band", None, None),
        P("band", None),
        P("segment", None, None, None),
        P("segment", None),
        P("segment", None),
        P("segment", None),
        P("segment", None, None),
        P("segment", None),
        P("segment", None, None),
        P("segment", None),
    )
    return jax.shard_map(
        on_device, mesh=mesh, in_specs=in_specs,
        out_specs=P("segment", None, "band", None, None), check_vma=False,
    )
```

```python
import jax
import jax.numpy as jnp
from jax import lax
from jax.experimental import pallas as pl
from jax.experimental.pallas import tpu as pltpu
from jax.sharding import PartitionSpec as P

BF, F32 = jnp.bfloat16, jnp.float32
MESH = pl.DeviceIdType.MESH
KS, REACH = 7, 3
R, W, C, HID = 16, 64, 256, 1024
BLOCKS, DATES, BANDS = 4, 2, 64
PIECES = 8
UPR, DNR = C // PIECES, HID // PIECES
CH = 4
NCH = R // CH


def tree(p):
    return ((p[0] + p[1]) + (p[2] + p[3])) + ((p[4] + p[5]) + p[6])


def conv_row(state, taps, sp, normed, i, part):
    half = W // 2
    for h in range(2):
        xs = [state[i + a, h * half:(h + 1) * half].reshape(half // 8, 8, C) for a in range(KS)]
        for b in range(KS):
            t = tree([xs[a] * taps[a * KS + b][None] for a in range(KS)])
            t = t.astype(F32).reshape(half, C)
            for l in range(2):
                tl = t[:, l * 128:(l + 1) * 128]
                part[b, l, 8 + h * half:8 + (h + 1) * half, :] = tl
                if h == 0 and b > REACH:
                    part[b, l, 8 + W:16 + W, :] = tl[0:8]
                if h == 1 and b < REACH:
                    part[b, l, 0:8, :] = tl[half - 8:half]
    sums = []
    for l in range(2):
        acc = sp[0:1, l * 128:(l + 1) * 128]
        for b in range(KS):
            acc = acc + part[b, l, 8 + b - REACH:8 + b - REACH + W, :]
        sums.append(acc)
    mean = jnp.sum(sums[0] + sums[1], -1, keepdims=True) * (1.0 / C)
    dev = [x - mean for x in sums]
    var = jnp.sum(dev[0] * dev[0] + dev[1] * dev[1], -1, keepdims=True) * (1.0 / C)
    scale = lax.rsqrt(var + 1e-6)
    out = jnp.concatenate(
        [dev[l] * scale * sp[1:2, l * 128:(l + 1) * 128] + sp[2:3, l * 128:(l + 1) * 128]
         for l in range(2)], axis=1)
    normed[pl.ds(pl.multiple_of(i * W, W), W), :] = out.astype(BF)


def mlp_chunk(normed, state, result, mask, up, dn, sp, hid, ck):
    m = CH * W
    r0 = pl.multiple_of(ck * m, m)
    n = normed[pl.ds(r0, m), :]
    for j in range(4):
        js = slice(j * 256, (j + 1) * 256)
        h = jnp.dot(n, up[:, js], preferred_element_type=F32) + sp[4:5, js]
        v = h.astype(BF)
        e = lax.erf(v * jnp.asarray(0.7071067811865476, BF))
        hid[:, js] = v + v * e
    u = jnp.dot(hid[...], dn[...], preferred_element_type=F32) * 0.5 + sp[3:4, 0:C]
    st = state[pl.ds(ck * CH + REACH, CH)].reshape(m, C).astype(F32)
    mk = mask[pl.ds(r0, m), :]
    o = (st + u) * jnp.concatenate([mk, mk], axis=1)
    result[pl.ds(ck * CH + REACH, CH)] = o.astype(BF).reshape(CH, W, C)


def kernel(fields, land, ck, cb, ng, ns, up, ub, dn, db, out,
           S, WU, WD, CK, SP, TP, N, H, MK, PT,
           f_sem, own_sem, y_send, k_send, k_recv, w_recv, x_send, c_send,
           h_send, h_recv, o_send, o_recv, l_sem):
    band, q = lax.axis_index("band"), lax.axis_index("segment")
    core = lax.rem(band, 2)
    xpos = band // 16
    sib = band + 1 - 2 * core
    other = jnp.where(core == 0, band - 1, band + 1)
    has_prev, has_next = band > 0, band < BANDS - 1
    has_other = jnp.logical_and(other >= 0, other < BANDS)
    mine = 2 * xpos + core

    def at(b, s):
        return {"band": b, "segment": s}

    def x_band(k):
        return lax.rem(band + 16 * k, BANDS)

    def seg(r):
        return lax.rem(q + r, BLOCKS)

    barrier = pltpu.get_barrier_semaphore()

    def greet(b, s):
        pl.semaphore_signal(barrier, inc=1, device_id=at(b, s), device_id_type=MESH)

    for r in (1, 2, 3):
        greet(band, seg(r))
    for k in (1, 2, 3):
        greet(x_band(k), q)
    greet(sib, q)

    @pl.when(has_other)
    def _():
        greet(other, q)

    def field_copy(d):
        return pltpu.make_async_copy(
            fields.at[DATES * q + d], S.at[d, 0, pl.ds(REACH, R)], f_sem.at[d])

    field_copy(0).start()
    field_copy(1).start()
    own_up = pltpu.make_async_copy(up.at[0], WU.at[q], own_sem.at[0])
    own_dn = pltpu.make_async_copy(dn.at[0], WD.at[q], own_sem.at[1])
    own_up.start()
    own_dn.start()

    CK[q] = ck[0]
    SP[q, 0:1, 0:C] = cb[...].astype(F32)
    SP[q, 1:2, 0:C] = ng[...].astype(F32)
    SP[q, 2:3, 0:C] = ns[...].astype(F32)
    SP[q, 3:4, 0:C] = db[...].astype(F32)
    SP[q, 4:5, :] = ub[...].astype(F32)

    eye = (lax.broadcasted_iota(jnp.int32, (W, W), 0)
           == lax.broadcasted_iota(jnp.int32, (W, W), 1))

    @pl.loop(0, R)
    def _(i):
        row = jnp.broadcast_to(land[pl.ds(i, 1), :].astype(F32), (W, W))
        col = jnp.sum(jnp.where(eye, row, 0.0), -1, keepdims=True)
        MK[pl.ds(pl.multiple_of(i * W, W), W), :] = jnp.broadcast_to(col, (W, 128))

    edge = jnp.zeros((REACH, W, C), BF)

    @pl.when(jnp.logical_not(has_prev))
    def _():
        @pl.loop(0, DATES * BLOCKS)
        def _(t):
            S[t // BLOCKS, lax.rem(t, BLOCKS), 0:REACH] = edge

    @pl.when(jnp.logical_not(has_next))
    def _():
        @pl.loop(0, DATES * BLOCKS)
        def _(t):
            S[t // BLOCKS, lax.rem(t, BLOCKS), R + REACH:R + 2 * REACH] = edge

    pl.semaphore_wait(barrier, 7 + has_other.astype(jnp.int32))

    def k_copies(r, s):
        return (
            pltpu.make_async_remote_copy(
                CK.at[s], CK.at[s], k_send.at[r - 1, 0], k_recv.at[s, 0],
                device_id=at(band, seg(r)), device_id_type=MESH),
            pltpu.make_async_remote_copy(
                SP.at[s], SP.at[s], k_send.at[r - 1, 1], k_recv.at[s, 1],
                device_id=at(band, seg(r)), device_id_type=MESH))

    def part(ref, s, p, w):
        n = (UPR, DNR)[w]
        return ref.at[s, pl.ds(pl.multiple_of(p * n, n), n)]

    def y_copy(r, w):
        return pltpu.make_async_remote_copy(
            part((up, dn)[w], 0, mine, w), part((WU, WD)[w], q, mine, w),
            y_send.at[r - 1, w], w_recv.at[q, mine, w],
            device_id=at(band, seg(r)), device_id_type=MESH)

    def w_copy(s, p, w, b, sem):
        ref = (WU, WD)[w]
        return pltpu.make_async_remote_copy(
            part(ref, s, p, w), part(ref, s, p, w), sem, w_recv.at[s, p, w],
            device_id=at(b, q), device_id_type=MESH)

    def x_copy(s, k, w):
        return w_copy(s, mine, w, x_band(k), x_send.at[s, k - 1, w])

    def c_copy(s, k, w):
        p = 2 * lax.rem(xpos + k, 4) + core
        return w_copy(s, p, w, sib, c_send.at[s, k, w])

    for r in (1, 3, 2):
        for c in k_copies(r, q):
            c.start()
    for w in (0, 1):
        for r in (1, 3, 2):
            y_copy(r, w).start()

    def stage_x(s):
        @pl.when(q != s)
        def _():
            for w in (0, 1):
                c_copy(s, 0, w).wait_recv()
                for k in (1, 3, 2):
                    x_copy(s, k, w).start()
                c_copy(s, 0, w).start()

    def stage_c(s):
        @pl.when(q != s)
        def _():
            for w in (0, 1):
                for k in (1, 3, 2):
                    c_copy(s, k, w).wait_recv()
                    c_copy(s, k, w).start()

    def stage_f(s):
        @pl.when(q != s)
        def _():
            for w in (0, 1):
                for k in range(4):
                    p = 2 * k + 1 - core
                    w_copy(s, p, w, sib, c_send.at[s, k, w]).wait_recv()

        @pl.when(q == s)
        def _():
            own_up.wait()
            own_dn.wait()

    def halo(d, s, side):
        src = pl.ds(REACH, REACH) if side == 0 else pl.ds(R, REACH)
        dst = pl.ds(R + REACH, REACH) if side == 0 else pl.ds(0, REACH)
        to = band - 1 if side == 0 else band + 1
        return pltpu.make_async_remote_copy(
            S.at[d, s, src], S.at[d, s, dst], h_send.at[d, s, side], h_recv.at[d, s, side],
            device_id=at(to, q), device_id_type=MESH)

    def halo_start(d, s):
        @pl.when(has_prev)
        def _():
            halo(d, s, 0).start()

        @pl.when(has_next)
        def _():
            halo(d, s, 1).start()

    def halo_wait(d, s):
        @pl.when(has_next)
        def _():
            halo(d, s, 0).wait_recv()

        @pl.when(has_prev)
        def _():
            halo(d, s, 1).wait_recv()

    def halo_done(d, s):
        @pl.when(has_prev)
        def _():
            halo(d, s, 0).wait_send()

        @pl.when(has_next)
        def _():
            halo(d, s, 1).wait_send()

    for d in range(DATES):
        field_copy(d).wait()

        @pl.loop(0, R)
        def _(i):
            m = MK[pl.ds(pl.multiple_of(i * W, W), W), :]
            x = S[d, 0, i + REACH].astype(F32) * jnp.concatenate([m, m], axis=1)
            S[d, 0, i + REACH] = x.astype(BF)

        halo_start(d, 0)

    def rows(ref, ck):
        return ref.at[pl.ds(ck * CH, CH)]

    def o_copy(d, s, ck):
        return pltpu.make_async_remote_copy(
            S.at[d, s + 1, pl.ds(REACH + ck * CH, CH)],
            out.at[0, DATES * q + d, pl.ds(ck * CH, CH)],
            o_send.at[d, s, ck], o_recv.at[DATES * q + d, ck],
            device_id=at(band, s), device_id_type=MESH)

    def l_copy(d, s, ck):
        return pltpu.make_async_copy(
            S.at[d, s + 1, pl.ds(REACH + ck * CH, CH)],
            out.at[0, DATES * q + d, pl.ds(ck * CH, CH)], l_sem.at[d, ck])

    def send_out(d, s, ck):
        @pl.when(q != s)
        def _():
            o_copy(d, s, ck).start()

        @pl.when(q == s)
        def _():
            l_copy(d, s, ck).start()

    def order(t):
        return jnp.where(t == 1, NCH - 1, jnp.where(t > 1, t - 1, 0))

    def taps_of(s):
        @pl.when(q != s)
        def _():
            for w in (0, 1):
                pltpu.make_async_remote_copy(
                    (CK, SP)[w].at[s], (CK, SP)[w].at[s], k_send.at[0, w], k_recv.at[s, w],
                    device_id=at(band, seg(1)), device_id_type=MESH).wait_recv()

        @pl.loop(0, KS)
        def _(a):
            line = CK[s, a].astype(F32)
            for b in range(KS):
                TP[s, a * KS + b] = jnp.broadcast_to(line[b:b + 1], (8, C)).astype(BF)

    def conv_inner(d, s):
        @pl.loop(0, 5)
        def _(t):
            for k in range(2):
                conv_row(S.at[d, s], TP.at[s], SP.at[s], N.at[d], 2 * t + 3 + k, PT.at[k])

    def conv_outer(d, s):
        @pl.loop(0, 3)
        def _(t):
            for k in range(2):
                conv_row(S.at[d, s], TP.at[s], SP.at[s], N.at[d], t + 13 * k, PT.at[k])

    def mlp(d, s):
        @pl.loop(0, NCH)
        def _(t):
            mlp_chunk(N.at[d], S.at[d, s], S.at[d, s + 1], MK, WU.at[s], WD.at[s], SP.at[s], H, order(t))

            @pl.when(jnp.logical_and(t == 1, s < BLOCKS - 1))
            def _():
                halo_start(d, s + 1)

            @pl.when(t > 0)
            def _():
                send_out(d, s, order(t - 1))

            @pl.when(jnp.logical_and(t == 1, jnp.logical_and(d == 0, s < BLOCKS - 2)))
            def _():
                stage_x(s + 2)

        send_out(d, s, order(NCH - 1))

    taps_of(0)

    @pl.loop(0, DATES)
    def _(d):
        conv_inner(d, 0)
        halo_wait(d, 0)
        conv_outer(d, 0)

        @pl.when(d == 0)
        def _():
            stage_x(0)

    stage_x(1)
    stage_c(0)
    stage_f(0)

    @pl.loop(0, DATES)
    def _(d):
        mlp(d, 0)

    @pl.loop(2, DATES * BLOCKS)
    def _(unit):
        late = unit > BLOCKS
        d = jnp.where(late, 1, 0)
        s = jnp.where(late, unit - BLOCKS, unit - 1)

        @pl.when(d == 0)
        def _():
            taps_of(s)

        conv_inner(d, s)

        @pl.when(d == 0)
        def _():
            stage_c(s)

        halo_wait(d, s)
        conv_outer(d, s)

        @pl.when(d == 0)
        def _():
            stage_f(s)

        mlp(d, s)

    for r in (1, 2, 3):
        for c in k_copies(r, q):
            c.wait_send()
        for w in (0, 1):
            y_copy(r, w).wait_send()

    @pl.loop(0, BLOCKS)
    def _(s):
        @pl.when(q != s)
        def _():
            for w in (0, 1):
                for k in (1, 2, 3):
                    x_copy(s, k, w).wait_send()
                for k in range(4):
                    c_copy(s, k, w).wait_send()

        for d in range(DATES):
            halo_done(d, s)

            @pl.when(q != s)
            def _():
                for t in range(NCH):
                    o_copy(d, s, t).wait_send()

            @pl.when(q == s)
            def _():
                for t in range(NCH):
                    l_copy(d, s, t).wait()

        @pl.when(q != s)
        def _():
            for d in range(DATES):
                for t in range(NCH):
                    pltpu.make_async_remote_copy(
                        S.at[d, 1, pl.ds(REACH + t * CH, CH)],
                        out.at[0, DATES * s + d, pl.ds(t * CH, CH)],
                        o_send.at[d, 0, t], o_recv.at[DATES * s + d, t],
                        device_id=at(band, s), device_id_type=MESH).wait_recv()


def on_device(*args):
    args = [pltpu.with_memory_space_constraint(a, pltpu.HBM) if i in (0, 6, 8) else a
            for i, a in enumerate(args)]
    any_, vmem, hbm = pl.BlockSpec(memory_space=pl.ANY), pl.BlockSpec(memory_space=pltpu.VMEM), pl.BlockSpec(memory_space=pltpu.HBM)
    dma = pltpu.SemaphoreType.DMA
    return pl.pallas_call(
        kernel,
        out_shape=jax.ShapeDtypeStruct((1, DATES * BLOCKS, R, W, C), BF),
        in_specs=[hbm, vmem, vmem, vmem, vmem, vmem, hbm, vmem, hbm, vmem],
        out_specs=any_,
        scratch_shapes=[
            pltpu.VMEM((DATES, BLOCKS + 1, R + 2 * REACH, W, C), BF),
            pltpu.VMEM((BLOCKS, C, HID), BF),
            pltpu.VMEM((BLOCKS, HID, C), BF),
            pltpu.VMEM((BLOCKS, KS, KS, C), BF),
            pltpu.VMEM((BLOCKS, 8, HID), F32),
            pltpu.VMEM((BLOCKS, KS * KS, 8, C), BF),
            pltpu.VMEM((DATES, R * W, C), BF),
            pltpu.VMEM((CH * W, HID), BF),
            pltpu.VMEM((R * W, 128), F32),
            pltpu.VMEM((2, KS, 2, W + 16, 128), F32),
            dma((DATES,)),
            dma((2,)),
            dma((3, 2)),
            dma((3, 2)),
            dma((BLOCKS, 2)),
            dma((BLOCKS, PIECES, 2)),
            dma((BLOCKS, 3, 2)),
            dma((BLOCKS, 4, 2)),
            dma((DATES, BLOCKS, 2)),
            dma((DATES, BLOCKS, 2)),
            dma((DATES, BLOCKS, NCH)),
            dma((DATES * BLOCKS, NCH)),
            dma((DATES, NCH)),
        ],
        compiler_params=pltpu.CompilerParams(
            collective_id=0, has_side_effects=True, vmem_limit_bytes=24 << 20),
        name="blocks",
    )(*args)


def solution(mesh):
    in_specs = (
        P(None, "band", None, None),
        P("band", None),
        P("segment", None, None, None),
        P("segment", None),
        P("segment", None),
        P("segment", None),
        P("segment", None, None),
        P("segment", None),
        P("segment", None, None),
        P("segment", None),
    )
    return jax.shard_map(
        on_device, mesh=mesh, in_specs=in_specs,
        out_specs=P("segment", None, "band", None, None), check_vma=False,
    )
```

```python
import jax
import jax.numpy as jnp
from jax import lax
from jax.experimental import pallas as pl
from jax.experimental.pallas import tpu as pltpu
from jax.sharding import PartitionSpec as P

BF, F32 = jnp.bfloat16, jnp.float32
MESH = pl.DeviceIdType.MESH
KS, REACH = 7, 3
R, W, C, HID = 16, 64, 256, 1024
BLOCKS, DATES, BANDS = 4, 2, 64
PIECES = 8
UPR, DNR = C // PIECES, HID // PIECES
CH = 4
NCH = R // CH


def tree(p):
    return ((p[0] + p[1]) + (p[2] + p[3])) + ((p[4] + p[5]) + p[6])


def conv_row(state, taps, sp, shift, normed, i):
    half = W // 2
    parts = [[], [], [], [], [], [], []]
    for h in range(2):
        xs = [state[i + a, h * half:(h + 1) * half].reshape(half // 8, 8, C) for a in range(KS)]
        for b in range(KS):
            t = tree([xs[a] * taps[a * KS + b][None] for a in range(KS)])
            parts[b].append(t.reshape(half, C))
    stacked = jnp.concatenate([p for two in parts for p in two], axis=0)
    summed = jnp.dot(shift[...], stacked, preferred_element_type=F32) + sp[0:1, 0:C]
    mean = jnp.sum(summed, -1, keepdims=True) * (1.0 / C)
    dev = summed - mean
    var = jnp.sum(dev * dev, -1, keepdims=True) * (1.0 / C)
    out = dev * lax.rsqrt(var + 1e-6) * sp[1:2, 0:C] + sp[2:3, 0:C]
    normed[pl.ds(pl.multiple_of(i * W, W), W), :] = out.astype(BF)


def chunk(normed, state, result, mask, up, dn, taps, sp, shift, hid, ck, after):
    m = CH * W
    if after is not None:
        ahead = after * CH
    if ck is None:
        for j in range(CH):
            conv_row(state, taps, sp, shift, normed, ahead + j)
        return
    r0 = pl.multiple_of(ck * m, m)
    n = normed[pl.ds(r0, m), :]
    old = state[pl.ds(ck * CH + REACH, CH)]
    for j in range(CH):
        if after is not None:
            conv_row(state, taps, sp, shift, normed, ahead + j)
        js = slice(j * 256, (j + 1) * 256)
        h = jnp.dot(n, up[:, js], preferred_element_type=F32) + sp[4:5, js]
        v = h.astype(BF)
        e = lax.erf(v * jnp.asarray(0.7071067811865476, BF))
        hid[:, js] = v + v * e
    u = jnp.dot(hid[...], dn[...], preferred_element_type=F32) * 0.5 + sp[3:4, 0:C]
    mk = mask[pl.ds(r0, m), :]
    o = (old.reshape(m, C).astype(F32) + u) * jnp.concatenate([mk, mk], axis=1)
    result[pl.ds(ck * CH + REACH, CH)] = o.astype(BF).reshape(CH, W, C)


def kernel(fields, land_in, ck_in, cb_in, ng_in, ns_in, up, ub_in, dn, db_in, out,
           S, WU, WD, CK, SP, TP, N, H, MK, SH,
           land, ck, cb, ng, ns, ub, db,
           f_sem, own_sem, y_send, k_send, k_recv, w_recv, x_send, c_send,
           h_send, h_recv, o_send, o_recv, l_sem, i_sem):
    band, q = lax.axis_index("band"), lax.axis_index("segment")
    core = lax.rem(band, 2)
    xpos = band // 16
    sib = band + 1 - 2 * core
    other = jnp.where(core == 0, band - 1, band + 1)
    has_prev, has_next = band > 0, band < BANDS - 1
    has_other = jnp.logical_and(other >= 0, other < BANDS)
    mine = 2 * xpos + core

    def at(b, s):
        return {"band": b, "segment": s}

    def x_band(k):
        return lax.rem(band + 16 * k, BANDS)

    def seg(r):
        return lax.rem(q + r, BLOCKS)

    barrier = pltpu.get_barrier_semaphore()

    def greet(b, s):
        pl.semaphore_signal(barrier, inc=1, device_id=at(b, s), device_id_type=MESH)

    for r in (1, 2, 3):
        greet(band, seg(r))
    for k in (1, 2, 3):
        greet(x_band(k), q)
    greet(sib, q)

    @pl.when(has_other)
    def _():
        greet(other, q)

    def field_copy(d):
        return pltpu.make_async_copy(
            fields.at[DATES * q + d], S.at[d, 0, pl.ds(REACH, R)], f_sem.at[d])

    smalls = [pltpu.make_async_copy(a, b, i_sem.at[n]) for n, (a, b) in enumerate((
        (ck_in, ck), (cb_in, cb), (ng_in, ng), (ns_in, ns), (db_in, db), (ub_in, ub),
        (land_in, land)))]
    for c in smalls:
        c.start()
    field_copy(0).start()
    field_copy(1).start()
    own_up = pltpu.make_async_copy(up.at[0], WU.at[q], own_sem.at[0])
    own_dn = pltpu.make_async_copy(dn.at[0], WD.at[q], own_sem.at[1])
    own_up.start()
    own_dn.start()

    row_w = lax.broadcasted_iota(jnp.int32, (W, KS * W), 0)
    col = lax.broadcasted_iota(jnp.int32, (W, KS * W), 1)
    hit = ((row_w + (col >> 6) + (W - REACH)) & (W - 1)) == (col & (W - 1))
    SH[...] = jnp.where(hit, 1.0, 0.0).astype(BF)
    for c in smalls:
        c.wait()
    CK[q] = ck[0]
    SP[q, 0:1, 0:C] = cb[...].astype(F32)
    SP[q, 1:2, 0:C] = ng[...].astype(F32)
    SP[q, 2:3, 0:C] = ns[...].astype(F32)
    SP[q, 3:4, 0:C] = db[...].astype(F32)
    SP[q, 4:5, :] = ub[...].astype(F32)

    eye = (lax.broadcasted_iota(jnp.int32, (W, W), 0)
           == lax.broadcasted_iota(jnp.int32, (W, W), 1))

    @pl.loop(0, R)
    def _(i):
        row = jnp.broadcast_to(land[pl.ds(i, 1), :].astype(F32), (W, W))
        col = jnp.sum(jnp.where(eye, row, 0.0), -1, keepdims=True)
        MK[pl.ds(pl.multiple_of(i * W, W), W), :] = jnp.broadcast_to(col, (W, 128))

    edge = jnp.zeros((REACH, W, C), BF)

    @pl.when(jnp.logical_not(has_prev))
    def _():
        @pl.loop(0, DATES * BLOCKS)
        def _(t):
            S[t // BLOCKS, lax.rem(t, BLOCKS), 0:REACH] = edge

    @pl.when(jnp.logical_not(has_next))
    def _():
        @pl.loop(0, DATES * BLOCKS)
        def _(t):
            S[t // BLOCKS, lax.rem(t, BLOCKS), R + REACH:R + 2 * REACH] = edge

    pl.semaphore_wait(barrier, 7 + has_other.astype(jnp.int32))

    def k_copies(r, s):
        return (
            pltpu.make_async_remote_copy(
                CK.at[s], CK.at[s], k_send.at[r - 1, 0], k_recv.at[s, 0],
                device_id=at(band, seg(r)), device_id_type=MESH),
            pltpu.make_async_remote_copy(
                SP.at[s], SP.at[s], k_send.at[r - 1, 1], k_recv.at[s, 1],
                device_id=at(band, seg(r)), device_id_type=MESH))

    def part(ref, s, p, w):
        n = (UPR, DNR)[w]
        return ref.at[s, pl.ds(pl.multiple_of(p * n, n), n)]

    def y_copy(r, w):
        return pltpu.make_async_remote_copy(
            part((up, dn)[w], 0, mine, w), part((WU, WD)[w], q, mine, w),
            y_send.at[r - 1, w], w_recv.at[q, mine, w],
            device_id=at(band, seg(r)), device_id_type=MESH)

    def w_copy(s, p, w, b, sem):
        ref = (WU, WD)[w]
        return pltpu.make_async_remote_copy(
            part(ref, s, p, w), part(ref, s, p, w), sem, w_recv.at[s, p, w],
            device_id=at(b, q), device_id_type=MESH)

    def x_copy(s, k, w):
        return w_copy(s, mine, w, x_band(k), x_send.at[s, k - 1, w])

    def c_copy(s, k, w):
        p = 2 * lax.rem(xpos + k, 4) + core
        return w_copy(s, p, w, sib, c_send.at[s, k, w])

    for r in (1, 3, 2):
        for c in k_copies(r, q):
            c.start()
    def y_start():
        for w in (0, 1):
            for r in (1, 3, 2):
                y_copy(r, w).start()

    @pl.when(q == 0)
    def _():
        y_start()

    def stage_x(s):
        @pl.when(q != s)
        def _():
            for w in (0, 1):
                c_copy(s, 0, w).wait_recv()
                for k in (1, 3, 2):
                    x_copy(s, k, w).start()
                c_copy(s, 0, w).start()

    def stage_c(s):
        @pl.when(q != s)
        def _():
            for w in (0, 1):
                for k in (1, 3, 2):
                    c_copy(s, k, w).wait_recv()
                    c_copy(s, k, w).start()

    def stage_f(s):
        @pl.when(q != s)
        def _():
            for w in (0, 1):
                for k in range(4):
                    p = 2 * k + 1 - core
                    w_copy(s, p, w, sib, c_send.at[s, k, w]).wait_recv()

        @pl.when(q == s)
        def _():
            own_up.wait()
            own_dn.wait()

    def halo(d, s, side):
        src = pl.ds(REACH, REACH) if side == 0 else pl.ds(R, REACH)
        dst = pl.ds(R + REACH, REACH) if side == 0 else pl.ds(0, REACH)
        to = band - 1 if side == 0 else band + 1
        return pltpu.make_async_remote_copy(
            S.at[d, s, src], S.at[d, s, dst], h_send.at[d, s, side], h_recv.at[d, s, side],
            device_id=at(to, q), device_id_type=MESH)

    def halo_start(d, s, ck):
        @pl.when(jnp.logical_and(ck == 0, has_prev))
        def _():
            halo(d, s, 0).start()

        @pl.when(jnp.logical_and(ck == NCH - 1, has_next))
        def _():
            halo(d, s, 1).start()

    def halo_wait(d, s, ck):
        @pl.when(jnp.logical_and(ck == NCH - 1, has_next))
        def _():
            halo(d, s, 0).wait_recv()

        @pl.when(jnp.logical_and(ck == 0, has_prev))
        def _():
            halo(d, s, 1).wait_recv()

    def halo_done(d, s):
        @pl.when(has_prev)
        def _():
            halo(d, s, 0).wait_send()

        @pl.when(has_next)
        def _():
            halo(d, s, 1).wait_send()

    for d in range(DATES):
        field_copy(d).wait()

        @pl.loop(0, R)
        def _(i):
            m = MK[pl.ds(pl.multiple_of(i * W, W), W), :]
            x = S[d, 0, i + REACH].astype(F32) * jnp.concatenate([m, m], axis=1)
            S[d, 0, i + REACH] = x.astype(BF)

        halo_start(d, 0, 0)
        halo_start(d, 0, NCH - 1)

    @pl.when(q != 0)
    def _():
        y_start()

    def rows(ref, ck):
        return ref.at[pl.ds(ck * CH, CH)]

    def o_copy(d, s, ck):
        return pltpu.make_async_remote_copy(
            S.at[d, s + 1, pl.ds(REACH + ck * CH, CH)],
            out.at[0, DATES * q + d, pl.ds(ck * CH, CH)],
            o_send.at[d, s, ck], o_recv.at[DATES * q + d, ck],
            device_id=at(band, s), device_id_type=MESH)

    def l_copy(d, s, ck):
        return pltpu.make_async_copy(
            S.at[d, s + 1, pl.ds(REACH + ck * CH, CH)],
            out.at[0, DATES * q + d, pl.ds(ck * CH, CH)], l_sem.at[d, ck])

    def send_out(d, s, ck):
        @pl.when(q != s)
        def _():
            o_copy(d, s, ck).start()

        @pl.when(q == s)
        def _():
            l_copy(d, s, ck).start()

    def order(s, t):
        odd = lax.rem(s, 2) * (NCH - 1)
        return jnp.where(t == 0, 1, jnp.where(t == 1, odd, jnp.where(t == 2, NCH - 1 - odd, 2)))

    def taps_of(s):
        @pl.when(q != s)
        def _():
            for w in (0, 1):
                pltpu.make_async_remote_copy(
                    (CK, SP)[w].at[s], (CK, SP)[w].at[s], k_send.at[0, w], k_recv.at[s, w],
                    device_id=at(band, seg(1)), device_id_type=MESH).wait_recv()

        @pl.loop(0, KS)
        def _(a):
            line = CK[s, a].astype(F32)
            for b in range(KS):
                TP[s, a * KS + b] = jnp.broadcast_to(line[b:b + 1], (8, C)).astype(BF)

    def step(d, s, ck, after):
        chunk(N.at[d], S.at[d, s], S.at[d, s + 1], MK, WU.at[s], WD.at[s], TP.at[s], SP.at[s], SH, H,
              ck, after)

    def conv(d, s, t):
        ck = order(s, t)
        halo_wait(d, s, ck)
        step(d, s, None, ck)

    def finish(d, s, t):
        ck = order(s, t)

        @pl.when(s < BLOCKS - 1)
        def _():
            halo_start(d, s + 1, ck)

        @pl.when(t > 0)
        def _():
            send_out(d, s, order(s, t - 1))

        @pl.when(jnp.logical_and(t == 2, jnp.logical_and(d == 0, s < BLOCKS - 2)))
        def _():
            stage_x(s + 2)

        @pl.when(t == NCH - 1)
        def _():
            send_out(d, s, ck)

    taps_of(0)

    @pl.loop(0, DATES * NCH)
    def _(i):
        d, t = i // NCH, lax.rem(i, NCH)
        conv(d, 0, t)

        @pl.when(i == NCH - 1)
        def _():
            stage_x(0)

    stage_x(1)
    stage_c(0)
    stage_f(0)

    @pl.loop(0, DATES * NCH)
    def _(i):
        d, t = i // NCH, lax.rem(i, NCH)
        step(d, 0, order(0, t), None)
        finish(d, 0, t)

    @pl.loop(2, DATES * BLOCKS)
    def _(unit):
        late = unit > BLOCKS
        d = jnp.where(late, 1, 0)
        s = jnp.where(late, unit - BLOCKS, unit - 1)

        @pl.when(d == 0)
        def _():
            taps_of(s)

        conv(d, s, 0)

        @pl.when(d == 0)
        def _():
            stage_c(s)
            stage_f(s)

        @pl.loop(0, NCH - 1)
        def _(t):
            ck, after = order(s, t), order(s, t + 1)
            halo_wait(d, s, after)
            step(d, s, ck, after)
            finish(d, s, t)

        step(d, s, order(s, NCH - 1), None)
        finish(d, s, NCH - 1)

    for r in (1, 2, 3):
        for c in k_copies(r, q):
            c.wait_send()
        for w in (0, 1):
            y_copy(r, w).wait_send()

    @pl.loop(0, BLOCKS)
    def _(s):
        @pl.when(q != s)
        def _():
            for w in (0, 1):
                for k in (1, 2, 3):
                    x_copy(s, k, w).wait_send()
                for k in range(4):
                    c_copy(s, k, w).wait_send()

        for d in range(DATES):
            halo_done(d, s)

            @pl.when(q != s)
            def _():
                for t in range(NCH):
                    o_copy(d, s, t).wait_send()

            @pl.when(q == s)
            def _():
                for t in range(NCH):
                    l_copy(d, s, t).wait()

        @pl.when(q != s)
        def _():
            for d in range(DATES):
                for t in range(NCH):
                    pltpu.make_async_remote_copy(
                        S.at[d, 1, pl.ds(REACH + t * CH, CH)],
                        out.at[0, DATES * s + d, pl.ds(t * CH, CH)],
                        o_send.at[d, 0, t], o_recv.at[DATES * s + d, t],
                        device_id=at(band, s), device_id_type=MESH).wait_recv()


def on_device(*args):
    args = [pltpu.with_memory_space_constraint(a, pltpu.HBM) for a in args]
    any_, hbm = pl.BlockSpec(memory_space=pl.ANY), pl.BlockSpec(memory_space=pltpu.HBM)
    dma = pltpu.SemaphoreType.DMA
    return pl.pallas_call(
        kernel,
        out_shape=jax.ShapeDtypeStruct((1, DATES * BLOCKS, R, W, C), BF),
        in_specs=[hbm] * 10,
        out_specs=any_,
        scratch_shapes=[
            pltpu.VMEM((DATES, BLOCKS + 1, R + 2 * REACH, W, C), BF),
            pltpu.VMEM((BLOCKS, C, HID), BF),
            pltpu.VMEM((BLOCKS, HID, C), BF),
            pltpu.VMEM((BLOCKS, KS, KS, C), BF),
            pltpu.VMEM((BLOCKS, 8, HID), F32),
            pltpu.VMEM((BLOCKS, KS * KS, 8, C), BF),
            pltpu.VMEM((DATES, R * W, C), BF),
            pltpu.VMEM((CH * W, HID), BF),
            pltpu.VMEM((R * W, 128), F32),
            pltpu.VMEM((W, KS * W), BF),
            pltpu.VMEM((R, W), jnp.int32),
            pltpu.VMEM((1, KS, KS, C), BF),
            pltpu.VMEM((1, C), BF),
            pltpu.VMEM((1, C), BF),
            pltpu.VMEM((1, C), BF),
            pltpu.VMEM((1, HID), BF),
            pltpu.VMEM((1, C), BF),
            dma((DATES,)),
            dma((2,)),
            dma((3, 2)),
            dma((3, 2)),
            dma((BLOCKS, 2)),
            dma((BLOCKS, PIECES, 2)),
            dma((BLOCKS, 3, 2)),
            dma((BLOCKS, 4, 2)),
            dma((DATES, BLOCKS, 2)),
            dma((DATES, BLOCKS, 2)),
            dma((DATES, BLOCKS, NCH)),
            dma((DATES * BLOCKS, NCH)),
            dma((DATES, NCH)),
            dma((7,)),
        ],
        compiler_params=pltpu.CompilerParams(
            collective_id=0, has_side_effects=True, vmem_limit_bytes=24 << 20),
        name="blocks",
    )(*args)


def solution(mesh):
    in_specs = (
        P(None, "band", None, None),
        P("band", None),
        P("segment", None, None, None),
        P("segment", None),
        P("segment", None),
        P("segment", None),
        P("segment", None, None),
        P("segment", None),
        P("segment", None, None),
        P("segment", None),
    )
    return jax.shard_map(
        on_device, mesh=mesh, in_specs=in_specs,
        out_specs=P("segment", None, "band", None, None), check_vma=False,
    )
```

```python
import jax
import jax.numpy as jnp
from jax import lax
from jax.experimental import pallas as pl
from jax.experimental.pallas import tpu as pltpu
from jax.sharding import PartitionSpec as P

BF, F32 = jnp.bfloat16, jnp.float32
MESH = pl.DeviceIdType.MESH
KS, REACH = 7, 3
R, W, C, HID = 16, 64, 256, 1024
BLOCKS, DATES, BANDS = 4, 2, 64
PIECES = 8
UPR, DNR = C // PIECES, HID // PIECES
CH = 4
NCH = R // CH


def tree(p):
    return ((p[0] + p[1]) + (p[2] + p[3])) + ((p[4] + p[5]) + p[6])


def conv_row(state, taps, sp, shift, normed, i):
    half = W // 2
    parts = [[], [], [], [], [], [], []]
    for h in range(2):
        xs = [state[i + a, h * half:(h + 1) * half].reshape(half // 8, 8, C) for a in range(KS)]
        for b in range(KS):
            t = tree([xs[a] * taps[a * KS + b][None] for a in range(KS)])
            parts[b].append(t.reshape(half, C))
    stacked = jnp.concatenate([p for two in parts for p in two], axis=0)
    summed = jnp.dot(shift[...], stacked, preferred_element_type=F32) + sp[0:1, 0:C]
    mean = jnp.sum(summed, -1, keepdims=True) * (1.0 / C)
    dev = summed - mean
    var = jnp.sum(dev * dev, -1, keepdims=True) * (1.0 / C)
    out = dev * lax.rsqrt(var + 1e-6) * sp[1:2, 0:C] + sp[2:3, 0:C]
    normed[pl.ds(pl.multiple_of(i * W, W), W), :] = out.astype(BF)


def chunk(normed, state, result, mask, up, dn, taps, sp, shift, hid, ck, after):
    m = CH * W
    if after is not None:
        ahead = after * CH
    if ck is None:
        for j in range(CH):
            conv_row(state, taps, sp, shift, normed, ahead + j)
        return
    r0 = pl.multiple_of(ck * m, m)
    n = normed[pl.ds(r0, m), :]
    old = state[pl.ds(ck * CH + REACH, CH)]
    for j in range(CH):
        if after is not None:
            conv_row(state, taps, sp, shift, normed, ahead + j)
        js = slice(j * 256, (j + 1) * 256)
        h = jnp.dot(n, up[:, js], preferred_element_type=F32) + sp[4:5, js]
        v = h.astype(BF)
        e = lax.erf(v * jnp.asarray(0.7071067811865476, BF))
        hid[:, js] = v + v * e
    u = jnp.dot(hid[...], dn[...], preferred_element_type=F32) * 0.5 + sp[3:4, 0:C]
    mk = mask[pl.ds(r0, m), :]
    o = (old.reshape(m, C).astype(F32) + u) * jnp.concatenate([mk, mk], axis=1)
    result[pl.ds(ck * CH + REACH, CH)] = o.astype(BF).reshape(CH, W, C)


def kernel(fields, land_in, ck_in, cb_in, ng_in, ns_in, up, ub_in, dn, db_in, out,
           S, WU, WD, CK, SP, TP, N, H, MK, SH,
           land, ck, cb, ng, ns, ub, db,
           f_sem, own_sem, y_send, k_send, k_recv, w_recv, x_send, c_send,
           h_send, h_recv, o_send, o_recv, l_sem, i_sem, RL, rl_send, rl_recv):
    band, q = lax.axis_index("band"), lax.axis_index("segment")
    core = lax.rem(band, 2)
    xpos = band // 16
    sib = band + 1 - 2 * core
    other = jnp.where(core == 0, band - 1, band + 1)
    has_prev, has_next = band > 0, band < BANDS - 1
    has_other = jnp.logical_and(other >= 0, other < BANDS)
    mine = 2 * xpos + core

    def at(b, s):
        return {"band": b, "segment": s}

    def x_band(k):
        return lax.rem(band + 16 * k, BANDS)

    def seg(r):
        return lax.rem(q + r, BLOCKS)

    barrier = pltpu.get_barrier_semaphore()

    def greet(b, s):
        pl.semaphore_signal(barrier, inc=1, device_id=at(b, s), device_id_type=MESH)

    for r in (1, 2, 3):
        greet(band, seg(r))
    for k in (1, 2, 3):
        greet(x_band(k), q)
    greet(sib, q)

    @pl.when(has_other)
    def _():
        greet(other, q)

    def field_copy(d):
        return pltpu.make_async_copy(
            fields.at[DATES * q + d], S.at[d, 0, pl.ds(REACH, R)], f_sem.at[d])

    smalls = [pltpu.make_async_copy(a, b, i_sem.at[n]) for n, (a, b) in enumerate((
        (ck_in, ck), (cb_in, cb), (ng_in, ng), (ns_in, ns), (db_in, db), (ub_in, ub),
        (land_in, land)))]
    for c in smalls:
        c.start()
    field_copy(0).start()
    field_copy(1).start()
    own_up = pltpu.make_async_copy(up.at[0], WU.at[q], own_sem.at[0])
    own_dn = pltpu.make_async_copy(dn.at[0], WD.at[q], own_sem.at[1])
    own_up.start()
    own_dn.start()

    row_w = lax.broadcasted_iota(jnp.int32, (W, KS * W), 0)
    col = lax.broadcasted_iota(jnp.int32, (W, KS * W), 1)
    hit = ((row_w + (col >> 6) + (W - REACH)) & (W - 1)) == (col & (W - 1))
    SH[...] = jnp.where(hit, 1.0, 0.0).astype(BF)
    for c in smalls:
        c.wait()
    CK[q] = ck[0]
    SP[q, 0:1, 0:C] = cb[...].astype(F32)
    SP[q, 1:2, 0:C] = ng[...].astype(F32)
    SP[q, 2:3, 0:C] = ns[...].astype(F32)
    SP[q, 3:4, 0:C] = db[...].astype(F32)
    SP[q, 4:5, :] = ub[...].astype(F32)

    eye = (lax.broadcasted_iota(jnp.int32, (W, W), 0)
           == lax.broadcasted_iota(jnp.int32, (W, W), 1))

    @pl.loop(0, R)
    def _(i):
        row = jnp.broadcast_to(land[pl.ds(i, 1), :].astype(F32), (W, W))
        col = jnp.sum(jnp.where(eye, row, 0.0), -1, keepdims=True)
        MK[pl.ds(pl.multiple_of(i * W, W), W), :] = jnp.broadcast_to(col, (W, 128))

    edge = jnp.zeros((REACH, W, C), BF)

    @pl.when(jnp.logical_not(has_prev))
    def _():
        @pl.loop(0, DATES * BLOCKS)
        def _(t):
            S[t // BLOCKS, lax.rem(t, BLOCKS), 0:REACH] = edge

    @pl.when(jnp.logical_not(has_next))
    def _():
        @pl.loop(0, DATES * BLOCKS)
        def _(t):
            S[t // BLOCKS, lax.rem(t, BLOCKS), R + REACH:R + 2 * REACH] = edge

    pl.semaphore_wait(barrier, 7 + has_other.astype(jnp.int32))

    def k_copies(r, s):
        return (
            pltpu.make_async_remote_copy(
                CK.at[s], CK.at[s], k_send.at[r - 1, 0], k_recv.at[s, 0],
                device_id=at(band, seg(r)), device_id_type=MESH),
            pltpu.make_async_remote_copy(
                SP.at[s], SP.at[s], k_send.at[r - 1, 1], k_recv.at[s, 1],
                device_id=at(band, seg(r)), device_id_type=MESH))

    def part(ref, s, p, w):
        n = (UPR, DNR)[w]
        return ref.at[s, pl.ds(pl.multiple_of(p * n, n), n)]

    def y_copy(r, w):
        return pltpu.make_async_remote_copy(
            part((up, dn)[w], 0, mine, w), part((WU, WD)[w], q, mine, w),
            y_send.at[r - 1, w], w_recv.at[q, mine, w],
            device_id=at(band, seg(r)), device_id_type=MESH)

    def w_copy(s, p, w, b, sem):
        ref = (WU, WD)[w]
        return pltpu.make_async_remote_copy(
            part(ref, s, p, w), part(ref, s, p, w), sem, w_recv.at[s, p, w],
            device_id=at(b, q), device_id_type=MESH)

    def x_copy(s, k, w):
        return w_copy(s, mine, w, x_band(k), x_send.at[s, k - 1, w])

    def c_copy(s, k, w):
        p = 2 * lax.rem(xpos + k, 4) + core
        return w_copy(s, p, w, sib, c_send.at[s, k, w])

    for r in (1, 3, 2):
        for c in k_copies(r, q):
            c.start()
    def y_start():
        for w in (0, 1):
            for r in (1, 3, 2):
                y_copy(r, w).start()

    @pl.when(q == 0)
    def _():
        y_start()

    def stage_x(s):
        @pl.when(q != s)
        def _():
            for w in (0, 1):
                c_copy(s, 0, w).wait_recv()
                for k in (1, 3, 2):
                    x_copy(s, k, w).start()
                c_copy(s, 0, w).start()

    def stage_c(s):
        @pl.when(q != s)
        def _():
            for w in (0, 1):
                for k in (1, 3, 2):
                    c_copy(s, k, w).wait_recv()
                    c_copy(s, k, w).start()

    def stage_f(s):
        @pl.when(q != s)
        def _():
            for w in (0, 1):
                for k in range(4):
                    p = 2 * k + 1 - core
                    w_copy(s, p, w, sib, c_send.at[s, k, w]).wait_recv()

        @pl.when(q == s)
        def _():
            own_up.wait()
            own_dn.wait()

    def halo(d, s, side):
        src = pl.ds(REACH, REACH) if side == 0 else pl.ds(R, REACH)
        dst = pl.ds(R + REACH, REACH) if side == 0 else pl.ds(0, REACH)
        to = band - 1 if side == 0 else band + 1
        return pltpu.make_async_remote_copy(
            S.at[d, s, src], S.at[d, s, dst], h_send.at[d, s, side], h_recv.at[d, s, side],
            device_id=at(to, q), device_id_type=MESH)

    def halo_start(d, s, ck):
        @pl.when(jnp.logical_and(ck == 0, has_prev))
        def _():
            halo(d, s, 0).start()

        @pl.when(jnp.logical_and(ck == NCH - 1, has_next))
        def _():
            halo(d, s, 1).start()

    def halo_wait(d, s, ck):
        @pl.when(jnp.logical_and(ck == NCH - 1, has_next))
        def _():
            halo(d, s, 0).wait_recv()

        @pl.when(jnp.logical_and(ck == 0, has_prev))
        def _():
            halo(d, s, 1).wait_recv()

    def halo_done(d, s):
        @pl.when(has_prev)
        def _():
            halo(d, s, 0).wait_send()

        @pl.when(has_next)
        def _():
            halo(d, s, 1).wait_send()

    for d in range(DATES):
        field_copy(d).wait()

        @pl.loop(0, R)
        def _(i):
            m = MK[pl.ds(pl.multiple_of(i * W, W), W), :]
            x = S[d, 0, i + REACH].astype(F32) * jnp.concatenate([m, m], axis=1)
            S[d, 0, i + REACH] = x.astype(BF)

        halo_start(d, 0, 0)
        halo_start(d, 0, NCH - 1)

    @pl.when(q != 0)
    def _():
        y_start()

    def rows(ref, ck):
        return ref.at[pl.ds(ck * CH, CH)]

    def o_copy(d, s, ck):
        return pltpu.make_async_remote_copy(
            S.at[d, s + 1, pl.ds(REACH + ck * CH, CH)],
            out.at[0, DATES * q + d, pl.ds(ck * CH, CH)],
            o_send.at[d, s, ck], o_recv.at[DATES * q + d, ck],
            device_id=at(band, s), device_id_type=MESH)

    def l_copy(d, s, ck):
        return pltpu.make_async_copy(
            S.at[d, s + 1, pl.ds(REACH + ck * CH, CH)],
            out.at[0, DATES * q + d, pl.ds(ck * CH, CH)], l_sem.at[d, ck])

    relayed = jnp.logical_and(q == 1, core == 1)
    relays = jnp.logical_and(q == 2, core == 1)

    def relay_in(d, ck):
        return pltpu.make_async_remote_copy(
            S.at[d, BLOCKS, pl.ds(REACH + ck * CH, CH)], RL.at[d, pl.ds(ck * CH, CH)],
            o_send.at[d, BLOCKS - 1, ck], rl_recv.at[d, ck],
            device_id=at(band, 2), device_id_type=MESH)

    def relay_out(d, ck):
        return pltpu.make_async_remote_copy(
            RL.at[d, pl.ds(ck * CH, CH)], out.at[0, DATES + d, pl.ds(ck * CH, CH)],
            rl_send.at[d, ck], o_recv.at[DATES + d, ck],
            device_id=at(band, BLOCKS - 1), device_id_type=MESH)

    def relay(d, ck):
        relay_in(d, ck).wait_recv()
        relay_out(d, ck).start()

    def send_out(d, s, ck):
        by_relay = jnp.logical_and(relayed, s == BLOCKS - 1)

        @pl.when(by_relay)
        def _():
            relay_in(d, ck).start()

        @pl.when(jnp.logical_and(q != s, jnp.logical_not(by_relay)))
        def _():
            o_copy(d, s, ck).start()

        @pl.when(q == s)
        def _():
            l_copy(d, s, ck).start()

    def order(s, t):
        odd = lax.rem(s, 2) * (NCH - 1)
        return jnp.where(t == 0, 1, jnp.where(t == 1, odd, jnp.where(t == 2, NCH - 1 - odd, 2)))

    def taps_of(s):
        @pl.when(q != s)
        def _():
            for w in (0, 1):
                pltpu.make_async_remote_copy(
                    (CK, SP)[w].at[s], (CK, SP)[w].at[s], k_send.at[0, w], k_recv.at[s, w],
                    device_id=at(band, seg(1)), device_id_type=MESH).wait_recv()

        @pl.loop(0, KS)
        def _(a):
            line = CK[s, a].astype(F32)
            for b in range(KS):
                TP[s, a * KS + b] = jnp.broadcast_to(line[b:b + 1], (8, C)).astype(BF)

    def step(d, s, ck, after):
        chunk(N.at[d], S.at[d, s], S.at[d, s + 1], MK, WU.at[s], WD.at[s], TP.at[s], SP.at[s], SH, H,
              ck, after)

    def conv(d, s, t):
        ck = order(s, t)
        halo_wait(d, s, ck)
        step(d, s, None, ck)

    def finish(d, s, t):
        ck = order(s, t)

        @pl.when(s < BLOCKS - 1)
        def _():
            halo_start(d, s + 1, ck)

        @pl.when(t > 0)
        def _():
            send_out(d, s, order(s, t - 1))

        @pl.when(jnp.logical_and(relays, jnp.logical_and(d == 1, s == 2)))
        def _():
            relay(0, order(BLOCKS - 1, t))

        @pl.when(t == NCH - 1)
        def _():
            send_out(d, s, ck)

    taps_of(0)

    @pl.loop(0, DATES * NCH)
    def _(i):
        d, t = i // NCH, lax.rem(i, NCH)
        conv(d, 0, t)

        @pl.when(i == NCH - 1)
        def _():
            stage_x(0)

    stage_x(1)
    stage_c(0)
    stage_f(0)
    stage_x(2)

    @pl.loop(0, DATES * NCH)
    def _(i):
        d, t = i // NCH, lax.rem(i, NCH)
        step(d, 0, order(0, t), None)
        finish(d, 0, t)

        @pl.when(i == NCH + 1)
        def _():
            stage_c(1)

    stage_x(3)

    @pl.loop(2, DATES * BLOCKS)
    def _(unit):
        late = unit > BLOCKS
        d = jnp.where(late, 1, 0)
        s = jnp.where(late, unit - BLOCKS, unit - 1)

        @pl.when(d == 0)
        def _():
            taps_of(s)

        conv(d, s, 0)

        @pl.when(d == 0)
        def _():
            stage_f(s)

        @pl.loop(0, NCH - 1)
        def _(t):
            ck, after = order(s, t), order(s, t + 1)
            halo_wait(d, s, after)
            step(d, s, ck, after)
            finish(d, s, t)

        step(d, s, order(s, NCH - 1), None)
        finish(d, s, NCH - 1)

        @pl.when(jnp.logical_and(d == 0, s < BLOCKS - 1))
        def _():
            stage_c(s + 1)

    @pl.when(relays)
    def _():
        for t in range(NCH):
            relay(1, order(BLOCKS - 1, t))

    for r in (1, 2, 3):
        for c in k_copies(r, q):
            c.wait_send()
        for w in (0, 1):
            y_copy(r, w).wait_send()

    @pl.when(relays)
    def _():
        for d in range(DATES):
            for t in range(NCH):
                relay_out(d, t).wait_send()

    @pl.loop(0, BLOCKS)
    def _(s):
        @pl.when(q != s)
        def _():
            for w in (0, 1):
                for k in (1, 2, 3):
                    x_copy(s, k, w).wait_send()
                for k in range(4):
                    c_copy(s, k, w).wait_send()

        for d in range(DATES):
            halo_done(d, s)

            @pl.when(q != s)
            def _():
                for t in range(NCH):
                    o_copy(d, s, t).wait_send()

            @pl.when(q == s)
            def _():
                for t in range(NCH):
                    l_copy(d, s, t).wait()

        @pl.when(q != s)
        def _():
            for d in range(DATES):
                for t in range(NCH):
                    pltpu.make_async_remote_copy(
                        S.at[d, 1, pl.ds(REACH + t * CH, CH)],
                        out.at[0, DATES * s + d, pl.ds(t * CH, CH)],
                        o_send.at[d, 0, t], o_recv.at[DATES * s + d, t],
                        device_id=at(band, s), device_id_type=MESH).wait_recv()


def on_device(*args):
    args = [pltpu.with_memory_space_constraint(a, pltpu.HBM) for a in args]
    any_, hbm = pl.BlockSpec(memory_space=pl.ANY), pl.BlockSpec(memory_space=pltpu.HBM)
    dma = pltpu.SemaphoreType.DMA
    return pl.pallas_call(
        kernel,
        out_shape=jax.ShapeDtypeStruct((1, DATES * BLOCKS, R, W, C), BF),
        in_specs=[hbm] * 10,
        out_specs=any_,
        scratch_shapes=[
            pltpu.VMEM((DATES, BLOCKS + 1, R + 2 * REACH, W, C), BF),
            pltpu.VMEM((BLOCKS, C, HID), BF),
            pltpu.VMEM((BLOCKS, HID, C), BF),
            pltpu.VMEM((BLOCKS, KS, KS, C), BF),
            pltpu.VMEM((BLOCKS, 8, HID), F32),
            pltpu.VMEM((BLOCKS, KS * KS, 8, C), BF),
            pltpu.VMEM((DATES, R * W, C), BF),
            pltpu.VMEM((CH * W, HID), BF),
            pltpu.VMEM((R * W, 128), F32),
            pltpu.VMEM((W, KS * W), BF),
            pltpu.VMEM((R, W), jnp.int32),
            pltpu.VMEM((1, KS, KS, C), BF),
            pltpu.VMEM((1, C), BF),
            pltpu.VMEM((1, C), BF),
            pltpu.VMEM((1, C), BF),
            pltpu.VMEM((1, HID), BF),
            pltpu.VMEM((1, C), BF),
            dma((DATES,)),
            dma((2,)),
            dma((3, 2)),
            dma((3, 2)),
            dma((BLOCKS, 2)),
            dma((BLOCKS, PIECES, 2)),
            dma((BLOCKS, 3, 2)),
            dma((BLOCKS, 4, 2)),
            dma((DATES, BLOCKS, 2)),
            dma((DATES, BLOCKS, 2)),
            dma((DATES, BLOCKS, NCH)),
            dma((DATES * BLOCKS, NCH)),
            dma((DATES, NCH)),
            dma((7,)),
            pltpu.VMEM((DATES, R, W, C), BF),
            dma((DATES, NCH)),
            dma((DATES, NCH)),
        ],
        compiler_params=pltpu.CompilerParams(
            collective_id=0, has_side_effects=True, vmem_limit_bytes=24 << 20),
        name="blocks",
    )(*args)


def solution(mesh):
    in_specs = (
        P(None, "band", None, None),
        P("band", None),
        P("segment", None, None, None),
        P("segment", None),
        P("segment", None),
        P("segment", None),
        P("segment", None, None),
        P("segment", None),
        P("segment", None, None),
        P("segment", None),
    )
    return jax.shard_map(
        on_device, mesh=mesh, in_specs=in_specs,
        out_specs=P("segment", None, "band", None, None), check_vma=False,
    )
```

```python
import jax
import jax.numpy as jnp
from jax import lax
from jax.experimental import pallas as pl
from jax.experimental.pallas import tpu as pltpu
from jax.sharding import PartitionSpec as P

BF, F32 = jnp.bfloat16, jnp.float32
MESH = pl.DeviceIdType.MESH
KS, REACH = 7, 3
R, W, C, HID = 16, 64, 256, 1024
BLOCKS, DATES, BANDS = 4, 2, 64
PIECES = 8
UPR, DNR = C // PIECES, HID // PIECES
CH = 4
NCH = R // CH


def tree(p):
    return ((p[0] + p[1]) + (p[2] + p[3])) + ((p[4] + p[5]) + p[6])


def conv_row(state, taps, sp, shift, normed, i):
    half = W // 2
    parts = [[], [], [], [], [], [], []]
    for h in range(2):
        xs = [state[i + a, h * half:(h + 1) * half].reshape(half // 8, 8, C) for a in range(KS)]
        for b in range(KS):
            t = tree([xs[a] * taps[a * KS + b][None] for a in range(KS)])
            parts[b].append(t.reshape(half, C))
    stacked = jnp.concatenate([p for two in parts for p in two], axis=0)
    summed = jnp.dot(shift[...], stacked, preferred_element_type=F32) + sp[0:1, 0:C]
    mean = jnp.sum(summed, -1, keepdims=True) * (1.0 / C)
    dev = summed - mean
    var = jnp.sum(dev * dev, -1, keepdims=True) * (1.0 / C)
    out = dev * lax.rsqrt(var + 1e-6) * sp[1:2, 0:C] + sp[2:3, 0:C]
    normed[pl.ds(pl.multiple_of(i * W, W), W), :] = out.astype(BF)


def chunk(normed, state, result, mask, up, dn, taps, sp, shift, hid, ck, after):
    m = CH * W
    if after is not None:
        ahead = after * CH
    if ck is None:
        for j in range(CH):
            conv_row(state, taps, sp, shift, normed, ahead + j)
        return
    r0 = pl.multiple_of(ck * m, m)
    n = normed[pl.ds(r0, m), :]
    old = state[pl.ds(ck * CH + REACH, CH)]
    for j in range(CH):
        if after is not None:
            conv_row(state, taps, sp, shift, normed, ahead + j)
        js = slice(j * 256, (j + 1) * 256)
        h = jnp.dot(n, up[:, js], preferred_element_type=F32) + sp[4:5, js]
        v = h.astype(BF)
        e = lax.erf(v * jnp.asarray(0.7071067811865476, BF))
        hid[:, js] = v + v * e
    u = jnp.dot(hid[...], dn[...], preferred_element_type=F32) * 0.5 + sp[3:4, 0:C]
    mk = mask[pl.ds(r0, m), :]
    o = (old.reshape(m, C).astype(F32) + u) * jnp.concatenate([mk, mk], axis=1)
    result[pl.ds(ck * CH + REACH, CH)] = o.astype(BF).reshape(CH, W, C)


def kernel(fields, land_in, ck_in, cb_in, ng_in, ns_in, up, ub_in, dn, db_in, out,
           S, WU, WD, CK, SP, TP, N, H, MK, SH,
           land, ck, cb, ng, ns, ub, db,
           f_sem, own_sem, y_send, k_send, k_recv, w_recv, x_send, c_send,
           h_send, h_recv, o_send, o_recv, l_sem, i_sem):
    band, q = lax.axis_index("band"), lax.axis_index("segment")
    core = lax.rem(band, 2)
    xpos = band // 16
    sib = band + 1 - 2 * core
    other = jnp.where(core == 0, band - 1, band + 1)
    has_prev, has_next = band > 0, band < BANDS - 1
    has_other = jnp.logical_and(other >= 0, other < BANDS)
    mine = 2 * xpos + core

    def at(b, s):
        return {"band": b, "segment": s}

    def x_band(k):
        return lax.rem(band + 16 * k, BANDS)

    def seg(r):
        return lax.rem(q + r, BLOCKS)

    barrier = pltpu.get_barrier_semaphore()

    def greet(b, s):
        pl.semaphore_signal(barrier, inc=1, device_id=at(b, s), device_id_type=MESH)

    for r in (1, 2, 3):
        greet(band, seg(r))
    for k in (1, 2, 3):
        greet(x_band(k), q)
    greet(sib, q)

    @pl.when(has_other)
    def _():
        greet(other, q)

    def field_copy(d):
        return pltpu.make_async_copy(
            fields.at[DATES * q + d], S.at[d, 0, pl.ds(REACH, R)], f_sem.at[d])

    smalls = [pltpu.make_async_copy(a, b, i_sem.at[n]) for n, (a, b) in enumerate((
        (ck_in, ck), (cb_in, cb), (ng_in, ng), (ns_in, ns), (db_in, db), (ub_in, ub),
        (land_in, land)))]
    for c in smalls:
        c.start()
    field_copy(0).start()
    field_copy(1).start()
    own_up = pltpu.make_async_copy(up.at[0], WU.at[q], own_sem.at[0])
    own_dn = pltpu.make_async_copy(dn.at[0], WD.at[q], own_sem.at[1])
    own_up.start()
    own_dn.start()

    def k_copies(r, s):
        return (
            pltpu.make_async_remote_copy(
                CK.at[s], CK.at[s], k_send.at[r - 1, 0], k_recv.at[s, 0],
                device_id=at(band, seg(r)), device_id_type=MESH),
            pltpu.make_async_remote_copy(
                SP.at[s], SP.at[s], k_send.at[r - 1, 1], k_recv.at[s, 1],
                device_id=at(band, seg(r)), device_id_type=MESH))

    def part(ref, s, p, w):
        n = (UPR, DNR)[w]
        return ref.at[s, pl.ds(pl.multiple_of(p * n, n), n)]

    def y_copy(r, w):
        return pltpu.make_async_remote_copy(
            part((up, dn)[w], 0, mine, w), part((WU, WD)[w], q, mine, w),
            y_send.at[r - 1, w], w_recv.at[q, mine, w],
            device_id=at(band, seg(r)), device_id_type=MESH)

    def w_copy(s, p, w, b, sem):
        ref = (WU, WD)[w]
        return pltpu.make_async_remote_copy(
            part(ref, s, p, w), part(ref, s, p, w), sem, w_recv.at[s, p, w],
            device_id=at(b, q), device_id_type=MESH)

    def x_copy(s, k, w):
        return w_copy(s, mine, w, x_band(k), x_send.at[s, k - 1, w])

    def c_copy(s, k, w):
        p = 2 * lax.rem(xpos + k, 4) + core
        return w_copy(s, p, w, sib, c_send.at[s, k, w])

    pl.semaphore_wait(barrier, 7 + has_other.astype(jnp.int32))

    def y_start():
        for w in (0, 1):
            for r in (1, 3, 2):
                y_copy(r, w).start()

    @pl.when(q == 0)
    def _():
        y_start()

    for c in smalls:
        c.wait()
    CK[q] = ck[0]
    SP[q, 0:1, 0:C] = cb[...].astype(F32)
    SP[q, 1:2, 0:C] = ng[...].astype(F32)
    SP[q, 2:3, 0:C] = ns[...].astype(F32)
    SP[q, 3:4, 0:C] = db[...].astype(F32)
    SP[q, 4:5, :] = ub[...].astype(F32)

    row_w = lax.broadcasted_iota(jnp.int32, (W, KS * W), 0)
    col = lax.broadcasted_iota(jnp.int32, (W, KS * W), 1)
    hit = ((row_w + (col >> 6) + (W - REACH)) & (W - 1)) == (col & (W - 1))
    SH[...] = jnp.where(hit, 1.0, 0.0).astype(BF)
    for r in (1, 3, 2):
        for c in k_copies(r, q):
            c.start()

    eye = (lax.broadcasted_iota(jnp.int32, (W, W), 0)
           == lax.broadcasted_iota(jnp.int32, (W, W), 1))

    for i in range(R):
        row = jnp.broadcast_to(land[i:i + 1, :].astype(F32), (W, W))
        line = jnp.sum(jnp.where(eye, row, 0.0), -1, keepdims=True)
        MK[i * W:(i + 1) * W, :] = jnp.broadcast_to(line, (W, 128))

    edge = jnp.zeros((REACH, W, C), BF)

    @pl.when(jnp.logical_not(has_prev))
    def _():
        @pl.loop(0, DATES * BLOCKS)
        def _(t):
            S[t // BLOCKS, lax.rem(t, BLOCKS), 0:REACH] = edge

    @pl.when(jnp.logical_not(has_next))
    def _():
        @pl.loop(0, DATES * BLOCKS)
        def _(t):
            S[t // BLOCKS, lax.rem(t, BLOCKS), R + REACH:R + 2 * REACH] = edge

    def stage_x(s, halves=(0, 1)):
        @pl.when(q != s)
        def _():
            for w in halves:
                c_copy(s, 0, w).wait_recv()
                for k in (1, 3, 2):
                    x_copy(s, k, w).start()
                c_copy(s, 0, w).start()

    def stage_c(s):
        @pl.when(q != s)
        def _():
            for w in (0, 1):
                for k in (1, 3, 2):
                    c_copy(s, k, w).wait_recv()
                    c_copy(s, k, w).start()

    def stage_f(s):
        @pl.when(q != s)
        def _():
            for w in (0, 1):
                for k in range(4):
                    p = 2 * k + 1 - core
                    w_copy(s, p, w, sib, c_send.at[s, k, w]).wait_recv()

        @pl.when(q == s)
        def _():
            own_up.wait()
            own_dn.wait()

    def halo(d, s, side):
        src = pl.ds(REACH, REACH) if side == 0 else pl.ds(R, REACH)
        dst = pl.ds(R + REACH, REACH) if side == 0 else pl.ds(0, REACH)
        to = band - 1 if side == 0 else band + 1
        return pltpu.make_async_remote_copy(
            S.at[d, s, src], S.at[d, s, dst], h_send.at[d, s, side], h_recv.at[d, s, side],
            device_id=at(to, q), device_id_type=MESH)

    def halo_start(d, s, ck):
        @pl.when(jnp.logical_and(ck == 0, has_prev))
        def _():
            halo(d, s, 0).start()

        @pl.when(jnp.logical_and(ck == NCH - 1, has_next))
        def _():
            halo(d, s, 1).start()

    def halo_wait(d, s, ck):
        @pl.when(jnp.logical_and(ck == NCH - 1, has_next))
        def _():
            halo(d, s, 0).wait_recv()

        @pl.when(jnp.logical_and(ck == 0, has_prev))
        def _():
            halo(d, s, 1).wait_recv()

    def halo_done(d, s):
        @pl.when(has_prev)
        def _():
            halo(d, s, 0).wait_send()

        @pl.when(has_next)
        def _():
            halo(d, s, 1).wait_send()

    for d in range(DATES):
        field_copy(d).wait()

        @pl.loop(0, R)
        def _(i):
            m = MK[pl.ds(pl.multiple_of(i * W, W), W), :]
            x = S[d, 0, i + REACH].astype(F32) * jnp.concatenate([m, m], axis=1)
            S[d, 0, i + REACH] = x.astype(BF)

        halo_start(d, 0, 0)
        halo_start(d, 0, NCH - 1)

    @pl.when(q != 0)
    def _():
        y_start()

    def rows(ref, ck):
        return ref.at[pl.ds(ck * CH, CH)]

    def o_copy(d, s, ck):
        return pltpu.make_async_remote_copy(
            S.at[d, s + 1, pl.ds(REACH + ck * CH, CH)],
            out.at[0, DATES * q + d, pl.ds(ck * CH, CH)],
            o_send.at[d, s, ck], o_recv.at[DATES * q + d, ck],
            device_id=at(band, s), device_id_type=MESH)

    def l_copy(d, s, ck):
        return pltpu.make_async_copy(
            S.at[d, s + 1, pl.ds(REACH + ck * CH, CH)],
            out.at[0, DATES * q + d, pl.ds(ck * CH, CH)], l_sem.at[d, ck])

    def send_out(d, s, ck):
        @pl.when(q != s)
        def _():
            o_copy(d, s, ck).start()

        @pl.when(q == s)
        def _():
            l_copy(d, s, ck).start()

    def order(s, t):
        odd = lax.rem(s, 2) * (NCH - 1)
        return jnp.where(t == 0, 1, jnp.where(t == 1, odd, jnp.where(t == 2, NCH - 1 - odd, 2)))

    def taps_of(s):
        @pl.when(q != s)
        def _():
            for w in (0, 1):
                pltpu.make_async_remote_copy(
                    (CK, SP)[w].at[s], (CK, SP)[w].at[s], k_send.at[0, w], k_recv.at[s, w],
                    device_id=at(band, seg(1)), device_id_type=MESH).wait_recv()

        @pl.loop(0, KS)
        def _(a):
            line = CK[s, a].astype(F32)
            for b in range(KS):
                TP[s, a * KS + b] = jnp.broadcast_to(line[b:b + 1], (8, C)).astype(BF)

    def step(d, s, ck, after):
        chunk(N.at[d], S.at[d, s], S.at[d, s + 1], MK, WU.at[s], WD.at[s], TP.at[s], SP.at[s], SH, H,
              ck, after)

    def conv(d, s, t):
        ck = order(s, t)
        halo_wait(d, s, ck)
        step(d, s, None, ck)

    def finish(d, s, t):
        ck = order(s, t)

        @pl.when(s < BLOCKS - 1)
        def _():
            halo_start(d, s + 1, ck)

        @pl.when(t > 0)
        def _():
            send_out(d, s, order(s, t - 1))

        @pl.when(jnp.logical_and(t == 2, jnp.logical_and(d == 0, s == 0)))
        def _():
            @pl.when(q == 3)
            def _():
                stage_x(2)

            stage_x(3)

        @pl.when(t == NCH - 1)
        def _():
            send_out(d, s, ck)

    taps_of(0)

    @pl.loop(0, DATES * NCH)
    def _(i):
        d, t = i // NCH, lax.rem(i, NCH)
        conv(d, 0, t)

        @pl.when(i == 0)
        def _():
            stage_x(0, (0,))

        @pl.when(i == 2)
        def _():
            stage_x(0, (1,))

        @pl.when(i == 5)
        def _():
            stage_x(1)

    @pl.when(q < 2)
    def _():
        stage_x(2)

    stage_c(0)
    stage_f(0)

    def matmuls(d, s):
        @pl.loop(0, NCH)
        def _(t):
            step(d, s, order(s, t), None)
            finish(d, s, t)

    matmuls(0, 0)
    stage_c(1)

    @pl.loop(2, DATES * BLOCKS)
    def _(unit):
        late = unit > BLOCKS
        d = jnp.where(late, 1, 0)
        s = jnp.where(late, unit - BLOCKS, unit - 1)

        @pl.when(d == 0)
        def _():
            taps_of(s)

        @pl.when(unit == BLOCKS + 1)
        def _():
            matmuls(1, 0)

        conv(d, s, 0)

        @pl.when(d == 0)
        def _():
            stage_f(s)

        @pl.loop(0, NCH - 1)
        def _(t):
            ck, after = order(s, t), order(s, t + 1)
            halo_wait(d, s, after)
            step(d, s, ck, after)
            finish(d, s, t)

        step(d, s, order(s, NCH - 1), None)
        finish(d, s, NCH - 1)

        @pl.when(jnp.logical_and(d == 0, s < BLOCKS - 1))
        def _():
            stage_c(s + 1)

    for r in (1, 2, 3):
        for c in k_copies(r, q):
            c.wait_send()
        for w in (0, 1):
            y_copy(r, w).wait_send()

    @pl.loop(0, BLOCKS)
    def _(s):
        @pl.when(q != s)
        def _():
            for w in (0, 1):
                for k in (1, 2, 3):
                    x_copy(s, k, w).wait_send()
                for k in range(4):
                    c_copy(s, k, w).wait_send()

        for d in range(DATES):
            halo_done(d, s)

            @pl.when(q != s)
            def _():
                for t in range(NCH):
                    o_copy(d, s, t).wait_send()

            @pl.when(q == s)
            def _():
                for t in range(NCH):
                    l_copy(d, s, t).wait()

        @pl.when(q != s)
        def _():
            for d in range(DATES):
                for t in range(NCH):
                    pltpu.make_async_remote_copy(
                        S.at[d, 1, pl.ds(REACH + t * CH, CH)],
                        out.at[0, DATES * s + d, pl.ds(t * CH, CH)],
                        o_send.at[d, 0, t], o_recv.at[DATES * s + d, t],
                        device_id=at(band, s), device_id_type=MESH).wait_recv()


def on_device(*args):
    args = [pltpu.with_memory_space_constraint(a, pltpu.HBM) for a in args]
    any_, hbm = pl.BlockSpec(memory_space=pl.ANY), pl.BlockSpec(memory_space=pltpu.HBM)
    dma = pltpu.SemaphoreType.DMA
    return pl.pallas_call(
        kernel,
        out_shape=jax.ShapeDtypeStruct((1, DATES * BLOCKS, R, W, C), BF),
        in_specs=[hbm] * 10,
        out_specs=any_,
        scratch_shapes=[
            pltpu.VMEM((DATES, BLOCKS + 1, R + 2 * REACH, W, C), BF),
            pltpu.VMEM((BLOCKS, C, HID), BF),
            pltpu.VMEM((BLOCKS, HID, C), BF),
            pltpu.VMEM((BLOCKS, KS, KS, C), BF),
            pltpu.VMEM((BLOCKS, 8, HID), F32),
            pltpu.VMEM((BLOCKS, KS * KS, 8, C), BF),
            pltpu.VMEM((DATES, R * W, C), BF),
            pltpu.VMEM((CH * W, HID), BF),
            pltpu.VMEM((R * W, 128), F32),
            pltpu.VMEM((W, KS * W), BF),
            pltpu.VMEM((R, W), jnp.int32),
            pltpu.VMEM((1, KS, KS, C), BF),
            pltpu.VMEM((1, C), BF),
            pltpu.VMEM((1, C), BF),
            pltpu.VMEM((1, C), BF),
            pltpu.VMEM((1, HID), BF),
            pltpu.VMEM((1, C), BF),
            dma((DATES,)),
            dma((2,)),
            dma((3, 2)),
            dma((3, 2)),
            dma((BLOCKS, 2)),
            dma((BLOCKS, PIECES, 2)),
            dma((BLOCKS, 3, 2)),
            dma((BLOCKS, 4, 2)),
            dma((DATES, BLOCKS, 2)),
            dma((DATES, BLOCKS, 2)),
            dma((DATES, BLOCKS, NCH)),
            dma((DATES * BLOCKS, NCH)),
            dma((DATES, NCH)),
            dma((7,)),
        ],
        compiler_params=pltpu.CompilerParams(
            collective_id=0, has_side_effects=True, vmem_limit_bytes=24 << 20),
        name="blocks",
    )(*args)


def solution(mesh):
    in_specs = (
        P(None, "band", None, None),
        P("band", None),
        P("segment", None, None, None),
        P("segment", None),
        P("segment", None),
        P("segment", None),
        P("segment", None, None),
        P("segment", None),
        P("segment", None, None),
        P("segment", None),
    )
    return jax.shard_map(
        on_device, mesh=mesh, in_specs=in_specs,
        out_specs=P("segment", None, "band", None, None), check_vma=False,
    )
```
